32 devices in a mesh: dp: 8 (over z, x), tensor: 4 (over y, core).
Axes of the slice: x: 2, y: 2, z: 4, core: 2. Of those that a mesh axis runs over, the one named last changes fastest.
Arguments:
- final_layer_states: bfloat16 [16384, 8192], P('dp', 'tensor'), may hold values from -64 to 64
- entry_rms_multiplier: float32 [8192], replicated, may hold values from 0.25 to 1.75
- group_sharpness: float32 [64], replicated, may hold values from 0.1 to 1
- ancestor_ids: int32 [16384], P('dp'), may hold values from 0 to 62, as said below
- proposal_matrix: bfloat16 [8192, 4096], P('dp', 'tensor'), may hold values from -0.0625 to 0.0625
- future_vectors: bfloat16 [16384, 4096], P('dp', 'tensor'), may hold values from -6 to 6
Outputs:
- predicted: bfloat16 [16384, 4096], P('dp', 'tensor')
- weight_grad: float32 [8192, 4096], P('dp', 'tensor')
The draws below stay inside these ranges and needn't reach their ends.
Inputs may be any that keep to these rules, and one draw needn't show every extreme that they name: `ancestor_ids`: within each aligned block of 64 tokens, a token's entry is the in-block index of its parent, smaller than its own in-block index; the block's first token has 0, and its last token's parent is the one just before it.
All inputs are finite; a program needn't handle non-finite values.
Results may differ from the reference program's by a relative error of at most 0.012.
Values may be sent and summed in bfloat16 or wider, within the bound.
A program may use at most 128 MiB of HBM per device.

```python
import math
import jax
import jax.numpy as jnp
from jax import lax

D = 8192
QUERY_GROUP_TOTAL = 64
PER_GROUP_DEPTH = 128
DOUT = 4096
BLOCK = 64
TOKENS = 16384


def draw_ancestor_ids(key, part):
    position = jnp.arange(TOKENS, dtype=jnp.int32) % BLOCK
    drawn_ints = jax.random.randint(key, (TOKENS,), 0, BLOCK, dtype=jnp.int32)
    chosen = drawn_ints % jnp.maximum(position, 1)
    return jnp.where(position == BLOCK - 1, position - 1, chosen).astype(jnp.int32)


def draw_final_layer_states(key, part):
    keys = jax.random.split(key, 3)
    position = jnp.arange(TOKENS, dtype=jnp.int32) % BLOCK
    blocks = TOKENS // BLOCK
    block_head = jax.random.randint(keys[1], (blocks,), 0, QUERY_GROUP_TOTAL, dtype=jnp.int32)
    block_amp = jax.random.uniform(keys[2], (blocks,), jnp.float32, 5.0, 9.0)
    token_head = jnp.repeat(block_head, BLOCK)
    token_amp = jnp.repeat(block_amp, BLOCK)
    feature_head = jnp.arange(D, dtype=jnp.int32) // PER_GROUP_DEPTH
    base = jnp.clip(jax.random.normal(keys[0], (TOKENS, D), jnp.float32), -6.0, 6.0)
    drawn = base
    earlier = jnp.roll(base, 1, axis=0)
    child = (position == BLOCK - 1)[:, None]
    special = (position >= BLOCK - 2)[:, None]
    in_head = feature_head[None, :] == token_head[:, None]
    focused = jnp.where(child, earlier + 0.15 * base, base) * token_amp[:, None]
    row = jnp.where(special, jnp.where(in_head, focused, 0.1 * base), drawn)
    return jnp.clip(row, -64.0, 64.0).astype(jnp.bfloat16)


def steps_of(key, extent, cuts, least, largest):
    def one(dim, shards_of):
        draws = jax.random.uniform(jax.random.fold_in(jax.random.fold_in(key, 6), dim), (shards_of,), jnp.float32, least / len(cuts), largest / len(cuts))
        return jnp.repeat(jnp.exp(draws), extent[dim] // shards_of).reshape((-1,) + (1,) * (len(extent) - dim - 1))

    gain = one(*cuts[0])
    for cut in cuts[1:]:
        gain = gain * one(*cut)
    return gain


def noise(stream_key, extent, scale, bound, pieces=(), kind=jnp.bfloat16):
    drawn = scale * jax.random.normal(stream_key, extent, jnp.float32)
    if pieces:
        drawn = drawn * steps_of(stream_key, extent, pieces, -0.22, 0.18)
    return jnp.clip(drawn, -bound, bound).astype(kind)


def setup_inputs(seed: int = 0) -> dict:
    seeds = jax.random.split(jax.random.key(seed), 7)
    final_layer_states = draw_final_layer_states(jax.random.fold_in(seeds[6], 71), 0)
    entry_rms_multiplier = jnp.clip(1.0 + 0.15 * jax.random.normal(seeds[1], (D,), jnp.float32), 0.25, 1.75)
    group_sharpness = jnp.clip(jnp.exp(jax.random.uniform(seeds[2], (QUERY_GROUP_TOTAL,), jnp.float32, math.log(0.1), math.log(1.0))), 0.1, 1.0)
    ancestor_ids = draw_ancestor_ids(jax.random.fold_in(seeds[6], 71), 0)
    proposal_matrix = noise(seeds[4], (D, DOUT), D ** -0.5, 0.0625, ((0, 8), (1, 4)))
    future_vectors = noise(seeds[5], (TOKENS, DOUT), 1.0, 6.0, ((0, 8), (1, 4)))
    return {"final_layer_states": final_layer_states, "entry_rms_multiplier": entry_rms_multiplier, "group_sharpness": group_sharpness, "ancestor_ids": ancestor_ids, "proposal_matrix": proposal_matrix, "future_vectors": future_vectors}


def tree_reach(ancestor_ids):
    blocks = ancestor_ids.shape[0] // BLOCK
    index = jnp.arange(BLOCK, dtype=jnp.int32)
    grouped = ancestor_ids.reshape(blocks, BLOCK).astype(jnp.int32)
    link = ((grouped[:, :, None] == index[None, None, :]) & (index[None, :, None] > 0)).astype(jnp.float32)
    reach = link + jnp.eye(BLOCK, dtype=jnp.float32)[None]
    for sweep in range(6):
        reach = jnp.minimum(jnp.einsum('bts,bsu->btu', reach, reach, precision=lax.Precision.HIGHEST), 1.0)
    return reach

def branching_query_mixer(rescaled_entry, ancestor_ids, group_sharpness):
    rows = rescaled_entry.shape[0]
    blocks = rows // BLOCK
    reach = tree_reach(ancestor_ids)
    feats = rescaled_entry.reshape(blocks, BLOCK, QUERY_GROUP_TOTAL, PER_GROUP_DEPTH).astype(jnp.float32)
    softmax_multiplier = group_sharpness.astype(jnp.float32) / math.sqrt(PER_GROUP_DEPTH)
    scores = jnp.einsum('bthd,bshd->bhts', feats, feats) * softmax_multiplier[None, :, None, None]
    scores = jnp.where(reach[:, None] > 0, scores, -1e+30)
    top = lax.optimization_barrier(jnp.max(scores, axis=-1, keepdims=True))
    expd = jnp.exp(scores - top)
    probs = (expd / lax.optimization_barrier(jnp.sum(expd, axis=-1, keepdims=True))).astype(jnp.bfloat16)
    blended_result = jnp.einsum('bhts,bshd->bthd', probs.astype(jnp.float32), feats)
    return blended_result.astype(jnp.bfloat16).reshape(rows, QUERY_GROUP_TOTAL * PER_GROUP_DEPTH)

def reference(final_layer_states, entry_rms_multiplier, group_sharpness, ancestor_ids, proposal_matrix, future_vectors):
    wide_rows = final_layer_states.astype(jnp.float32)
    mean_sq = lax.optimization_barrier(jnp.mean(wide_rows * wide_rows, axis=1, keepdims=True))
    rescaled_entry = (wide_rows * lax.rsqrt(mean_sq + 1e-05) * entry_rms_multiplier[None, :]).astype(jnp.bfloat16)
    blended_result = branching_query_mixer(rescaled_entry, ancestor_ids, group_sharpness)
    projected = jnp.dot(blended_result, proposal_matrix, preferred_element_type=jnp.float32)
    predicted = projected.astype(jnp.bfloat16)
    residual_grad = jnp.clip(projected - future_vectors.astype(jnp.float32), -1.0, 1.0).astype(jnp.bfloat16)
    weight_grad = lax.dot_general(blended_result, residual_grad, (((0,), (0,)), ((), ())), preferred_element_type=jnp.float32)
    return (predicted, weight_grad / math.sqrt(TOKENS))
```

```python
import math

import jax
import jax.numpy as jnp
from jax import lax
from jax.experimental import pallas as pl
from jax.experimental.pallas import tpu as pltpu
from jax.sharding import PartitionSpec as P

PER_GROUP_DEPTH = 128
BLOCK = 64
PAIR = 2 * BLOCK
GROUPS = 4
STRIPS = 2
NEG = -1e30


def reach_kernel(ids_ref, bias_ref):
    count = ids_ref.shape[0]
    row = lax.broadcasted_iota(jnp.int32, (PAIR, PAIR), 0)
    col = lax.broadcasted_iota(jnp.int32, (PAIR, PAIR), 1)
    same = (row // BLOCK) == (col // BLOCK)
    eye = row == col
    reach = []
    for i in range(count):
        ids = ids_ref[i : i + 1, :]
        link = (ids == (row % BLOCK)) & ((col % BLOCK) > 0) & same
        reach.append(jnp.where(link | eye, 1.0, 0.0).astype(jnp.bfloat16))
    for sweep in range(6):
        for i in range(count):
            squared = jnp.dot(reach[i], reach[i], preferred_element_type=jnp.float32)
            reach[i] = jnp.minimum(squared, 1.0).astype(jnp.bfloat16)
    for i in range(count):
        bias_ref[i * PAIR : (i + 1) * PAIR, :] = jnp.where(reach[i].astype(jnp.float32) > 0, 0.0, NEG)


def reach_bias(ancestor_ids):
    rows = ancestor_ids.shape[0]
    pairs = rows // PAIR
    steps = 2
    return pl.pallas_call(
        reach_kernel,
        grid=(steps,),
        out_shape=jax.ShapeDtypeStruct((rows, PAIR), jnp.float32),
        in_specs=[pl.BlockSpec((pairs // steps, PAIR), lambda i: (i, 0))],
        out_specs=pl.BlockSpec((rows // steps, PAIR), lambda i: (i, 0)),
        cost_estimate=pl.CostEstimate(flops=rows * PAIR * PAIR * 12 * 8, bytes_accessed=rows * PAIR * 4, transcendentals=0),
        name="reach",
    )(ancestor_ids.reshape(pairs, PAIR))


def mix_kernel(x_ref, inv_ref, gain_ref, sharp_ref, bias_ref, out_ref):
    inv = inv_ref[...]
    heads = x_ref.shape[1] // PER_GROUP_DEPTH
    wave = min(4, heads)
    for first in range(0, heads, wave):
        span = range(first, first + wave)
        cut = [slice(h * PER_GROUP_DEPTH, (h + 1) * PER_GROUP_DEPTH) for h in span]
        feats = [(x_ref[:, c].astype(jnp.float32) * inv * gain_ref[:, c]).astype(jnp.bfloat16) for c in cut]
        scores = [
            lax.dot_general(f, f, (((1,), (1,)), ((), ())), preferred_element_type=jnp.float32) for f in feats
        ]
        probs = []
        for h, score in zip(span, scores):
            score = score * sharp_ref[0, h] + bias_ref[...]
            expd = jnp.exp(score - jnp.max(score, axis=0, keepdims=True))
            probs.append((expd * (1.0 / jnp.sum(expd, axis=0, keepdims=True))).astype(jnp.bfloat16))
        for c, prob, f in zip(cut, probs, feats):
            out_ref[:, c] = lax.dot_general(
                prob, f, (((0,), (0,)), ((), ())), preferred_element_type=jnp.float32
            ).astype(jnp.bfloat16)


def mix_group(group, states, inv, gain, sharp, bias):
    rows, width = states.shape
    rows_here = rows // GROUPS
    steps = rows_here // PAIR
    first = group * steps
    return pl.pallas_call(
        mix_kernel,
        grid=(steps,),
        out_shape=jax.ShapeDtypeStruct((rows_here, width), jnp.bfloat16),
        in_specs=[
            pl.BlockSpec((PAIR, width), lambda i: (i + first, 0)),
            pl.BlockSpec((PAIR, 1), lambda i: (i + first, 0)),
            pl.BlockSpec((1, width), lambda i: (0, 0)),
            pl.BlockSpec(memory_space=pltpu.SMEM),
            pl.BlockSpec((PAIR, PAIR), lambda i: (i + first, 0)),
        ],
        out_specs=pl.BlockSpec((PAIR, width), lambda i: (i, 0)),
        cost_estimate=pl.CostEstimate(
            flops=rows_here * width * PAIR * 4 * 8,
            bytes_accessed=rows_here * width * 4,
            transcendentals=rows_here * width,
        ),
        name="mix",
    )(states, inv, gain, sharp, bias)


def place_kernel(spots_ref, *refs):
    sources, out_ref = refs[:-1], refs[-1]
    width = sources[0].shape[1]
    pieces = spots_ref.shape[0] // len(sources)
    depth = width // pieces
    for i, source in enumerate(sources):
        for half in range(pieces):
            spot = pl.multiple_of(spots_ref[i * pieces + half] * depth, depth)
            out_ref[:, pl.ds(spot, depth)] = source[:, half * depth : (half + 1) * depth]


def place(spots, sources):
    rows, width = sources[0].shape
    full = width * len(sources)
    return pl.pallas_call(
        place_kernel,
        out_shape=jax.ShapeDtypeStruct((rows, full), sources[0].dtype),
        grid_spec=pltpu.PrefetchScalarGridSpec(
            num_scalar_prefetch=1,
            grid=(rows // PAIR,),
            in_specs=[pl.BlockSpec((PAIR, width), lambda i, spots: (i, 0)) for _ in sources],
            out_specs=pl.BlockSpec((PAIR, full), lambda i, spots: (i, 0)),
        ),
        cost_estimate=pl.CostEstimate(flops=0, bytes_accessed=rows * full * 4, transcendentals=0),
        name="place",
    )(spots, *sources)


def body(
    final_layer_states,
    entry_rms_multiplier,
    group_sharpness,
    ancestor_ids,
    proposal_matrix,
    future_vectors,
):
    tok_rows, col_count = final_layer_states.shape
    depth, out_cols = proposal_matrix.shape
    dp, tensor = lax.axis_size("dp"), lax.axis_size("tensor")
    width = col_count * tensor
    nz, outer = dp // 2, tensor // 2
    d = lax.axis_index("dp")
    z, x = d // 2, d % 2
    t = lax.axis_index("tensor")
    o, core = t // 2, t % 2
    x_perm = [(i, i ^ 1) for i in range(dp)]
    z_perm = [(i, (i + 2) % dp) for i in range(dp)]
    core_perm = [(i, i ^ 1) for i in range(tensor)]
    outer_perm = [(i, (i + 2) % tensor) for i in range(tensor)]

    flying = lax.ppermute(proposal_matrix, "dp", z_perm)
    crossing = lax.ppermute(proposal_matrix, "dp", x_perm)
    pieces = [proposal_matrix]

    bias = reach_bias(ancestor_ids)
    wide_rows = final_layer_states.astype(jnp.float32)
    squares = lax.psum(jnp.sum(wide_rows * wide_rows, axis=1), "tensor")
    inv = lax.rsqrt(squares[:, None] / width + 1e-05)
    own_gain = lax.dynamic_slice_in_dim(entry_rms_multiplier, t * col_count, col_count)[None, :]
    heads_here = col_count // PER_GROUP_DEPTH
    own_sharp = lax.dynamic_slice_in_dim(group_sharpness, t * heads_here, heads_here)[None, :]
    own_sharp = own_sharp / math.sqrt(PER_GROUP_DEPTH)

    per_source = col_count // depth
    spots = []
    for s in range(outer):
        for flip in range(2):
            source = lax.rem(o - s + outer, outer) * 2 + (core if flip == 0 else 1 - core)
            for half in range(per_source):
                j = source * per_source + half
                spots.append(lax.rem(z - j // 2 + nz, nz) * 2 + jnp.abs(j % 2 - x))
    spots = jnp.stack(spots).astype(jnp.int32)

    def advance(pieces, landed):
        pieces.append(landed[0])
        if len(landed) == 1:
            return None, None
        pieces.append(landed[1])
        further = None
        if len(pieces) < dp - 1:
            further = lax.ppermute(landed[1], "dp", z_perm)
        return further, lax.ppermute(landed[1], "dp", x_perm)

    rows_here = tok_rows // GROUPS
    lefts = []
    for g in range(GROUPS):
        current = mix_group(g, final_layer_states, inv, own_gain, own_sharp, bias)
        sources = []
        for s in range(outer):
            sources.append(current)
            sources.append(lax.ppermute(current, "tensor", core_perm))
            if s < outer - 1:
                current = lax.ppermute(current, "tensor", outer_perm)
                if s == outer - 2 and crossing is not None:
                    tied = lax.optimization_barrier((current, crossing) + (() if flying is None else (flying,)))
                    current = tied[0]
                    flying, crossing = advance(pieces, tied[1:])
        lefts.append(place(spots, sources))
    while crossing is not None:
        flying, crossing = advance(pieces, (crossing,) if flying is None else (crossing, flying))
    early = jnp.concatenate(pieces[:-1], axis=0)
    seam = early.shape[0]

    predicted, residuals = [], []
    for g, left in enumerate(lefts):
        projected = jnp.dot(left[:, :seam], early, preferred_element_type=jnp.float32)
        projected = projected + jnp.dot(left[:, seam:], pieces[-1], preferred_element_type=jnp.float32)
        target = future_vectors[g * rows_here : (g + 1) * rows_here].astype(jnp.float32)
        predicted.append(projected.astype(jnp.bfloat16))
        residuals.append(jnp.clip(projected - target, -1.0, 1.0).astype(jnp.bfloat16))
    residual = jnp.concatenate(residuals, axis=0)

    strip = out_cols // STRIPS

    def gradient(k, c):
        mixed = jnp.concatenate([left[:, k * depth : (k + 1) * depth] for left in lefts], axis=0)
        return lax.dot_general(
            mixed,
            residual[:, c * strip : (c + 1) * strip],
            (((0,), (0,)), ((), ())),
            preferred_element_type=jnp.float32,
        )

    ticks = nz * STRIPS
    order = [((i // STRIPS + 1) % nz * 2, i % STRIPS) for i in range(ticks)]
    away = [gradient(k + 1, c).astype(jnp.bfloat16) for k, c in order]
    keep = [lax.optimization_barrier(gradient(k, c)) for k, c in order]
    ahead = 2
    got = [lax.ppermute(piece, "dp", x_perm) for piece in away[:ahead]]
    arrived, totals = [None] * ticks, [None] * ticks
    for i in range(ticks):
        total = keep[i] + got[i].astype(jnp.float32)
        if i >= STRIPS:
            total = total + arrived[i - STRIPS].astype(jnp.float32)
        totals[i] = total
        if i < ticks - STRIPS:
            carry = total.astype(jnp.bfloat16)
            if i + ahead < ticks:
                carry, piece = lax.optimization_barrier((carry, away[i + ahead]))
                got.append(lax.ppermute(piece, "dp", x_perm))
            arrived[i] = lax.ppermute(carry, "dp", z_perm)
    totals = totals[-STRIPS:]
    weight_grad = jnp.concatenate(totals, axis=1) / math.sqrt(tok_rows * dp)
    return (jnp.concatenate(predicted, axis=0), weight_grad)


def solution(mesh):
    return jax.shard_map(
        body,
        mesh=mesh,
        in_specs=(P("dp", "tensor"), P(), P(), P("dp"), P("dp", "tensor"), P("dp", "tensor")),
        out_specs=(P("dp", "tensor"), P("dp", "tensor")),
        check_vma=False,
    )
```
